32 devices in a mesh: row: 4 (over z), col: 8 (over y, x, core).
Axes of the slice: x: 2, y: 2, z: 4, core: 2. Of those that a mesh axis runs over, the one named last changes fastest.
Arguments:
- normal_matrix: float32 [14336, 14336], P(('row', 'col')), may hold values from -90 to 90, as said below
- new_index: int32 [14336], replicated, may hold values from 0 to 14335, each once
- check_vectors: float32 [14336, 1024], P('col'), may hold values from -0.046875 to 0.046875
Outputs:
- tile_layout: float32 [14336, 14336], P('row', 'col')
- check_product: float32 [14336, 1024], P(('row', 'col'))
The draws below stay inside these ranges and needn't reach their ends.
Inputs may be any that keep to these rules, and one draw needn't show every extreme that they name: normal_matrix is symmetric. new_index[a] is the new index of parameter a; every index 0 to 14335 appears once.
All inputs are finite; a program needn't handle non-finite values.
Results may differ from the reference program's by a relative error of at most 0.000082.
Values sent between devices are 32-bit elements; how exact they have to be, the bound alone decides.
A program may use at most 192 MiB of HBM per device.

```python
import jax
import jax.numpy as jnp
from jax import lax

NPAR = 14336
TILE = 128
VECTORS = 1024
N_ROW = 4
N_COL = 8


def draw_normal_matrix(key, part):
    key_entries = jax.random.fold_in(key, 11)
    key_diagonal = jax.random.fold_in(key, 12)
    entries = jnp.clip(jax.random.normal(key_entries, (NPAR, NPAR), jnp.float32), -6.0, 6.0)
    symmetric = (entries + entries.T) * 0.7071
    diagonal_lift = jax.random.uniform(key_diagonal, (NPAR,), jnp.float32, 2.0, 8.0)
    return symmetric + jnp.diag(diagonal_lift)


def shard_levels(key, extent, split, smallest, largest):
    def one(dim, shards_of):
        steps = jax.random.uniform(jax.random.fold_in(jax.random.fold_in(key, 6), dim), (shards_of,), jnp.float32, smallest / len(split), largest / len(split))
        return jnp.repeat(jnp.exp(steps), extent[dim] // shards_of).reshape((-1,) + (1,) * (len(extent) - dim - 1))

    level = one(*split[0])
    for cut in split[1:]:
        level = level * one(*cut)
    return level


def scatter_about(own_key, extent, spread, most, pieces=(), kind=jnp.bfloat16):
    factor_of = shard_levels(own_key, extent, pieces, -0.22, 0.18) if pieces else 1.0
    array = jax.random.normal(own_key, extent, jnp.float32) * spread * factor_of
    return jnp.minimum(jnp.maximum(array, -most), most).astype(kind)


def setup_inputs(seed: int = 0) -> dict:
    key_list = jax.random.split(jax.random.key(seed), 4)
    return {
        "normal_matrix": draw_normal_matrix(jax.random.fold_in(key_list[3], 71), 0),
        "new_index": jax.random.permutation(key_list[1], NPAR).astype(jnp.int32),
        "check_vectors": scatter_about(key_list[2], (NPAR, VECTORS), NPAR ** -0.5, 0.046875, ((0, 8),), jnp.float32),
    }


def new_of_packed(places, groups, stride, tile_size):
    holder = places // stride
    within = places % stride
    return ((within // tile_size) * groups + holder) * tile_size + within % tile_size


def reference(normal_matrix, new_index, check_vectors):
    places = jnp.arange(NPAR, dtype=jnp.int32)
    old_of_new = jnp.zeros((NPAR,), jnp.int32).at[new_index].set(places)
    row_pick = old_of_new[new_of_packed(places, N_ROW, NPAR // N_ROW, TILE)]
    col_pick = old_of_new[new_of_packed(places, N_COL, NPAR // N_COL, TILE)]
    tile_layout = jnp.take(jnp.take(normal_matrix, row_pick, axis=0), col_pick, axis=1)
    check_product = jnp.dot(tile_layout, check_vectors, precision=lax.Precision.HIGHEST, preferred_element_type=jnp.float32)
    return tile_layout, check_product
```

```python
import jax
import jax.numpy as jnp
from jax import lax
from jax.sharding import PartitionSpec as P

TILE = 128
WIDTHS = 4


def inverse_of(new_index):
    unknowns = new_index.shape[0]
    tiles = unknowns // TILE
    places = jnp.arange(unknowns, dtype=jnp.int32)
    high = (new_index // TILE)[None, :] == jnp.arange(tiles, dtype=jnp.int32)[:, None]
    low = (new_index % TILE)[:, None] == jnp.arange(TILE, dtype=jnp.int32)[None, :]
    digits = jnp.concatenate(
        [
            jnp.where(low, (places // TILE)[:, None], 0).astype(jnp.bfloat16),
            jnp.where(low, (places % TILE)[:, None], 0).astype(jnp.bfloat16),
        ],
        axis=1,
    )
    found = jnp.dot(high.astype(jnp.bfloat16), digits, preferred_element_type=jnp.float32)
    found = found.astype(jnp.int32)
    return found[:, :TILE] * TILE + found[:, TILE:]


def cyclic(old_of_new, groups):
    tiles = old_of_new.shape[0]
    return old_of_new.reshape(tiles // groups, groups, TILE).transpose(1, 0, 2).reshape(-1)


def rows_of(matrix, picks):
    return matrix.at[picks].get(mode="promise_in_bounds", unique_indices=True)


def cuts_of(share):
    step = -(-share // WIDTHS)
    step = -(-step // 8) * 8
    return [(at, min(step, share - at)) for at in range(0, share, step)]


def shards(normal_matrix, new_index, check_vectors):
    row_count = lax.axis_size("row")
    col_count = lax.axis_size("col")
    devices = row_count * col_count
    unknowns = new_index.shape[0]
    slab_rows = normal_matrix.shape[0]
    share = unknowns // devices
    old_of_new = inverse_of(new_index)
    row_pick = cyclic(old_of_new, row_count).reshape(devices, share)
    col_pick = cyclic(old_of_new, col_count)
    turned = normal_matrix.T
    blocks, products = [], []
    for at, width in cuts_of(share):
        picks = row_pick[:, at : at + width].reshape(-1)
        outgoing = rows_of(turned, picks).reshape(devices, width, slab_rows)
        arrived = lax.all_to_all(outgoing, ("row", "col"), split_axis=0, concat_axis=0, tiled=True)
        by_old = arrived.transpose(0, 2, 1).reshape(unknowns, width)
        chosen = rows_of(by_old, col_pick).reshape(col_count, unknowns // col_count, width)
        moved = lax.all_to_all(chosen.transpose(0, 2, 1), "col", split_axis=0, concat_axis=0, tiled=True)
        blocks.append(moved)
        partial = jnp.dot(
            moved.reshape(col_count * width, -1),
            check_vectors,
            precision=lax.Precision.HIGH,
            preferred_element_type=jnp.float32,
        )
        products.append(lax.psum_scatter(partial, "col", scatter_dimension=0, tiled=True))
    tile_layout = jnp.concatenate(blocks, axis=1).reshape(col_count * share, -1)
    return (tile_layout, jnp.concatenate(products, axis=0))


def solution(mesh):
    return jax.shard_map(
        shards,
        mesh=mesh,
        in_specs=(P(("row", "col"), None), P(), P("col", None)),
        out_specs=(P("row", "col"), P(("row", "col"), None)),
        check_vma=False,
    )
```

```python
import jax
import jax.numpy as jnp
from jax import lax
from jax.sharding import PartitionSpec as P

TILE = 128
WIDTHS = 4


def inverse_of(new_index):
    unknowns = new_index.shape[0]
    tiles = unknowns // TILE
    places = jnp.arange(unknowns, dtype=jnp.int32)
    high = (new_index // TILE)[None, :] == jnp.arange(tiles, dtype=jnp.int32)[:, None]
    low = (new_index % TILE)[:, None] == jnp.arange(TILE, dtype=jnp.int32)[None, :]
    digits = jnp.concatenate(
        [
            jnp.where(low, (places // TILE)[:, None], 0).astype(jnp.bfloat16),
            jnp.where(low, (places % TILE)[:, None], 0).astype(jnp.bfloat16),
        ],
        axis=1,
    )
    found = jnp.dot(high.astype(jnp.bfloat16), digits, preferred_element_type=jnp.float32)
    found = found.astype(jnp.int32)
    return found[:, :TILE] * TILE + found[:, TILE:]


def cyclic(old_of_new, groups):
    tiles = old_of_new.shape[0]
    return old_of_new.reshape(tiles // groups, groups, TILE).transpose(1, 0, 2).reshape(-1)


def rows_of(matrix, picks):
    return matrix.at[picks].get(mode="promise_in_bounds", unique_indices=True)


def cuts_of(share):
    step = -(-2 * share // (2 * WIDTHS - 1))
    step = -(-step // 8) * 8
    return [(at, min(step, share - at)) for at in range(0, share, step)]


def exchange(pieces, col, count):
    held = jnp.zeros(pieces.shape, pieces.dtype)
    for step in range(count):
        piece = pieces[step]
        if step:
            piece = lax.ppermute(piece, "col", [(at, at ^ step) for at in range(count)])
        held = lax.dynamic_update_slice(held, piece[None], (col ^ step, 0, 0))
    return held


def shards(normal_matrix, new_index, check_vectors):
    row_count = lax.axis_size("row")
    col_count = lax.axis_size("col")
    devices = row_count * col_count
    unknowns = new_index.shape[0]
    slab_rows = normal_matrix.shape[0]
    share = unknowns // devices
    wide = unknowns // col_count
    col = lax.axis_index("col")
    old_of_new = inverse_of(new_index)
    row_pick = cyclic(old_of_new, row_count).reshape(devices, share)
    col_pick = cyclic(old_of_new, col_count)
    by_step = jnp.concatenate(
        [lax.dynamic_slice(col_pick, ((col ^ step) * wide,), (wide,)) for step in range(col_count)]
    )
    turned = normal_matrix.T
    tile_layout = jnp.zeros((col_count, share, wide), normal_matrix.dtype)
    partials, chosens, products = [], [], []
    cuts = cuts_of(share)

    def finish(chunk):
        moved = exchange(chosens[chunk], col, col_count)
        partials.append(
            jnp.dot(
                moved.reshape(-1, wide),
                check_vectors,
                precision=lax.Precision.HIGH,
                preferred_element_type=jnp.float32,
            )
        )
        return lax.dynamic_update_slice(tile_layout, moved, (0, cuts[chunk][0], 0))

    def after(value, chunk):
        held = ([chosens[chunk]] if chunk >= 0 else []) + ([partials[chunk - 1]] if chunk >= 1 else [])
        if held:
            value, *held = lax.optimization_barrier((value, *held))
            if chunk >= 1:
                partials[chunk - 1] = held.pop()
            chosens[chunk] = held.pop()
        return value

    for chunk, (at, width) in enumerate(cuts):
        picks = row_pick[:, at : at + width].reshape(-1)
        outgoing = rows_of(turned, picks).reshape(devices, width, slab_rows)
        outgoing = after(outgoing, chunk - 2)
        arrived = lax.all_to_all(outgoing, ("row", "col"), split_axis=0, concat_axis=0, tiled=True)
        if chunk == len(cuts) - 1:
            arrived = after(arrived, chunk - 1)
        by_old = arrived.transpose(0, 2, 1).reshape(unknowns, width)
        picked = rows_of(by_old, by_step)
        chosens.append(picked.reshape(col_count, wide, width).transpose(0, 2, 1))
        if chunk >= 1:
            tile_layout = finish(chunk - 1)
    tile_layout = finish(len(cuts) - 1)
    products = [lax.psum_scatter(part, "col", scatter_dimension=0, tiled=True) for part in partials]
    return (tile_layout.reshape(col_count * share, wide), jnp.concatenate(products, axis=0))


def solution(mesh):
    return jax.shard_map(
        shards,
        mesh=mesh,
        in_specs=(P(("row", "col"), None), P(), P("col", None)),
        out_specs=(P("row", "col"), P(("row", "col"), None)),
        check_vma=False,
    )
```
